32 devices in a mesh: seg: 8 (over z, x), par: 4 (over y, core).
Axes of the slice: x: 2, y: 2, z: 4, core: 2. Of those that a mesh axis runs over, the one named last changes fastest.
Arguments:
- points: bfloat16 [64, 128, 16384], P('seg', 'par'), may hold values from -9 to 9
- source_segment: int32 [64], P('seg'), may hold values from 0 to 62, as said below
- numerators: int32 [64], P('seg'), may hold values from 0 to 65535
Outputs:
- resampled: bfloat16 [64, 128, 16384], P('seg', 'par')
- arc: float32 [64], P('seg')
The draws below stay inside these ranges and needn't reach their ends.
Inputs may be any that keep to these rules, and one draw needn't show every extreme that they name: j - 3 <= source_segment[j] <= j + 2.
All inputs are finite; a program needn't handle non-finite values.
Results may differ from the reference program's by a relative error of at most 0.0017.
Values may be sent and summed in bfloat16 or wider, within the bound.
No kernel may reach another device: no remote copies, remote signals or barrier semaphores. Data moves between devices by JAX's collectives and lax.ppermute only.
A program may use at most 128 MiB of HBM per device.

```python
import jax
import jax.numpy as jnp
from jax import lax

FF = 16384
PTS_DEV = 8
NPTS = 64
ROWS = 128


def draw_points(key, part):
    key_values = jax.random.fold_in(key, 11)
    key_scales = jax.random.fold_in(key, 12)
    values = jnp.clip(jax.random.normal(key_values, (NPTS, ROWS, FF), jnp.float32), -4.0, 4.0)
    scales = jax.random.uniform(key_scales, (NPTS, 1, 1), jnp.float32, 0.75, 1.25)
    result = values * scales
    return jnp.clip(result, -9.0, 9.0).astype(jnp.bfloat16)


def draw_source_segment(key, part):
    offsets = jax.random.randint(jax.random.fold_in(key, 21), (NPTS,), -3, 3, jnp.int32)
    indices = jnp.arange(NPTS, dtype=jnp.int32)
    within = indices % PTS_DEV
    offsets = jnp.where(within == 0, -3, offsets).astype(jnp.int32)
    offsets = jnp.where(within == PTS_DEV - 1, 2, offsets).astype(jnp.int32)
    return jnp.clip(indices + offsets, 0, NPTS - 2).astype(jnp.int32)


def set_ends(values, rng, smallest, top_value):
    spot = [jax.random.randint(jax.random.fold_in(rng, axis), (), 0, length) for axis, length in enumerate(values.shape)]
    longest = values.shape.index(max(values.shape))
    neighbour = spot[:longest] + [(spot[longest] + 1) % values.shape[longest]] + spot[longest + 1:]
    return values.at[tuple(spot)].set(smallest).at[tuple(neighbour)].set(top_value)


def setup_inputs(seed: int = 0) -> dict:
    key_of = jax.random.split(jax.random.key(seed), 4)
    return {
        "points": draw_points(jax.random.fold_in(key_of[3], 71), 0),
        "source_segment": draw_source_segment(jax.random.fold_in(key_of[3], 71), 0),
        "numerators": set_ends(jax.random.randint(key_of[2], (NPTS,), 0, 65536), jax.random.fold_in(key_of[2], 1), 0, 65535).astype(jnp.int32),
    }


def segment_norm(points, position):
    start_point = lax.dynamic_index_in_dim(points, position, 0, keepdims=False).astype(jnp.float32)
    end_point = lax.dynamic_index_in_dim(points, position + 1, 0, keepdims=False).astype(jnp.float32)
    difference = end_point - start_point
    return jnp.sqrt(jnp.sum(difference * difference))

def reference(points, source_segment, numerators):
    positions = jnp.arange(NPTS - 1, dtype=jnp.int32)
    lengths = lax.map(lambda position: segment_norm(points, position), positions)
    arcs = jnp.concatenate([jnp.zeros((1,), jnp.float32), jnp.cumsum(lengths)])
    total = arcs[NPTS - 1]

    def place(pair):
        segment, numerator = pair
        target = total * (segment.astype(jnp.float32) + numerator.astype(jnp.float32) / 65536.0) / (NPTS - 1)
        fraction = (target - arcs[segment]) / lengths[segment]
        start_point = lax.dynamic_index_in_dim(points, segment, 0, keepdims=False).astype(jnp.float32)
        end_point = lax.dynamic_index_in_dim(points, segment + 1, 0, keepdims=False).astype(jnp.float32)
        return (start_point + fraction * (end_point - start_point)).astype(jnp.bfloat16)
    resampled = lax.map(place, (source_segment, numerators))
    return (resampled, arcs / total)
```

```python
import functools

import jax
import jax.numpy as jnp
from jax import lax
from jax.experimental import pallas as pl
from jax.experimental.pallas import tpu as pltpu
from jax.sharding import PartitionSpec as P


TILE_ROWS = 8
COL_BLOCKS = 4
LOW = 3


def place_kernel(
    chunk, n_own, rows, has_prev,
    buffer_rows, fractions, points, first, low, high, *rest
):
    if has_prev:
        rest = rest[1:]
    out, buf, res, in_sem, out_sem = rest
    width = points.shape[2]
    cols = width // COL_BLOCKS
    row0 = chunk * rows
    n_high = high.shape[0]

    def in_copies(c):
        at = pl.ds(c * cols, cols)
        own = pl.ds(row0, rows)
        pairs = (
            (points.at[:, own, at], buf.at[pl.ds(LOW, n_own), :, at]),
            (first.at[:, own, at], buf.at[pl.ds(LOW + n_own, 1), :, at]),
            (low.at[:, :, at], buf.at[pl.ds(0, LOW), :, at]),
            (high.at[:, :, at], buf.at[pl.ds(LOW + n_own + 1, n_high), :, at]),
        )
        return [
            pltpu.make_async_copy(src, dst, in_sem.at[c, k])
            for k, (src, dst) in enumerate(pairs)
        ]

    def out_copy(c):
        at = pl.ds(c * cols, cols)
        return pltpu.make_async_copy(
            res.at[:, :, at], out.at[:, pl.ds(row0, rows), at], out_sem.at[c]
        )

    for c in range(COL_BLOCKS):
        for copy in in_copies(c):
            copy.start()
    for c in range(COL_BLOCKS):
        for copy in in_copies(c):
            copy.wait()
        at = pl.ds(c * cols, cols)

        @pl.loop(0, n_own)
        def _(j):
            start = buf[buffer_rows[j], :, at].astype(jnp.float32)
            end = buf[buffer_rows[j] + 1, :, at].astype(jnp.float32)
            res[j, :, at] = (start + fractions[j] * (end - start)).astype(res.dtype)

        out_copy(c).start()
    for c in range(COL_BLOCKS):
        out_copy(c).wait()


def place(chunk, rows, buffer_rows, fractions, points, first, low, high, prev):
    n_own, _, width = points.shape
    held = LOW + n_own + 1 + high.shape[0]
    hbm = pl.BlockSpec(memory_space=pl.ANY)
    smem = pl.BlockSpec(memory_space=pltpu.SMEM)
    args = [buffer_rows, fractions, points, first, low, high]
    if prev is not None:
        args.append(prev)
    moved = (held + n_own) * rows * width * points.dtype.itemsize
    return pl.pallas_call(
        functools.partial(place_kernel, chunk, n_own, rows, prev is not None),
        out_shape=jax.ShapeDtypeStruct(points.shape, points.dtype),
        in_specs=[smem, smem] + [hbm] * (len(args) - 2),
        out_specs=hbm,
        scratch_shapes=[
            pltpu.VMEM((held, rows, width), points.dtype),
            pltpu.VMEM((n_own, rows, width), points.dtype),
            pltpu.SemaphoreType.DMA((COL_BLOCKS, 4)),
            pltpu.SemaphoreType.DMA((COL_BLOCKS,)),
        ],
        input_output_aliases={} if prev is None else {len(args) - 1: 0},
        cost_estimate=pl.CostEstimate(
            flops=4 * n_own * rows * width, bytes_accessed=moved, transcendentals=0
        ),
    )(*args)


def per_device(points, source_segment, numerators):
    n_own, n_rows, _ = points.shape
    device_index = lax.axis_index("seg")
    device_count = lax.axis_size("seg")
    first_point = device_index * n_own
    n_points = device_count * n_own
    forward = [(i, i + 1) for i in range(device_count - 1)]
    backward = [(b, a) for a, b in forward]
    rows = TILE_ROWS
    n_chunks = n_rows // rows

    first = lax.ppermute(points[:1], "seg", backward)
    lows, highs = [], []
    for c in range(n_chunks):
        at = slice(c * rows, (c + 1) * rows)
        lows.append(lax.ppermute(points[n_own - 3 :, at], "seg", forward))
        highs.append(lax.ppermute(points[1:3, at], "seg", backward))

    step = points[1:].astype(jnp.float32) - points[:-1].astype(jnp.float32)
    inner = jnp.sum(step * step, axis=(1, 2))
    step = first[0].astype(jnp.float32) - points[n_own - 1].astype(jnp.float32)
    edge = jnp.sum(step * step)
    partial = jnp.concatenate([inner, edge[None]])
    own_squares = lax.psum(partial, "par")
    squares = lax.all_gather(own_squares, "seg", axis=0, tiled=True)
    index = jnp.arange(n_points, dtype=jnp.int32)
    lengths = jnp.where(index < n_points - 1, jnp.sqrt(squares), 0.0)
    ends = jnp.cumsum(lengths)
    arcs = jnp.concatenate([jnp.zeros((1,), jnp.float32), ends[:-1]])
    total = arcs[n_points - 1]
    target = total * (
        source_segment.astype(jnp.float32) + numerators.astype(jnp.float32) / 65536.0
    ) / (n_points - 1)
    fractions = (target - arcs[source_segment]) / lengths[source_segment]
    arc = lax.dynamic_slice(arcs, (first_point,), (n_own,)) / total
    buffer_rows = source_segment - first_point + LOW

    out = None
    for c in range(n_chunks):
        out = place(
            c, rows, buffer_rows, fractions, points, first, lows[c], highs[c], out
        )
    return (out, arc)


def solution(mesh):
    return jax.shard_map(
        per_device,
        mesh=mesh,
        in_specs=(P("seg", "par", None), P("seg"), P("seg")),
        out_specs=(P("seg", "par", None), P("seg")),
        check_vma=False,
    )
```

```python
import functools

import jax
import jax.numpy as jnp
import numpy as np
from jax import lax
from jax.experimental import pallas as pl
from jax.experimental.pallas import tpu as pltpu
from jax.sharding import PartitionSpec as P


TILE_ROWS = 8
COL_BLOCKS = 4
LOW = 3
HIGH = 3
ROW, EDGE_ROW, AT_LOCAL, AT_EDGE, AT_FAR, RELAYED = range(6)


def place_kernel(
    rows, relays, has_prev,
    table, buffer_rows, fractions, points, edge, local, *rest
):
    fars, rest = rest[:relays], rest[relays:]
    if has_prev:
        rest = rest[1:]
    out, buf, res, in_sem, out_sem = rest
    n_own, _, width = points.shape
    cols = width // COL_BLOCKS
    row = pl.multiple_of(table[ROW], rows)
    edge_row = pl.multiple_of(table[EDGE_ROW], rows)

    def in_copy(c, k, far):
        at = pl.ds(c * cols, cols)
        src, start, count = (
            (points.at[:, pl.ds(row, rows), at], LOW, n_own),
            (edge.at[:, pl.ds(edge_row, rows), at], table[AT_EDGE], 1),
            (local.at[:, :, at], table[AT_LOCAL], local.shape[0]),
            (far.at[:, :, at], table[AT_FAR], far.shape[0]),
        )[k]
        dst = buf.at[pl.ds(start, count), :, at]
        return pltpu.make_async_copy(src, dst, in_sem.at[c, k])

    def out_copy(c):
        at = pl.ds(c * cols, cols)
        return pltpu.make_async_copy(
            res.at[:, :, at], out.at[:, pl.ds(row, rows), at], out_sem.at[c]
        )

    for c in range(COL_BLOCKS):
        for k in range(3):
            in_copy(c, k, fars[0]).start()
        if len(fars) == 1:
            in_copy(c, 3, fars[0]).start()
        else:

            @pl.when(table[RELAYED] == 1)
            def _():
                in_copy(c, 3, fars[1]).start()

            @pl.when(table[RELAYED] == 0)
            def _():
                in_copy(c, 3, fars[0]).start()

    for c in range(COL_BLOCKS):
        for k in range(4):
            in_copy(c, k, fars[0]).wait()
        at = pl.ds(c * cols, cols)

        @pl.loop(0, n_own)
        def _(j):
            start = buf[buffer_rows[j], :, at].astype(jnp.float32)
            end = buf[buffer_rows[j] + 1, :, at].astype(jnp.float32)
            res[j, :, at] = (start + fractions[j] * (end - start)).astype(res.dtype)

        out_copy(c).start()
    for c in range(COL_BLOCKS):
        out_copy(c).wait()


def place(rows, table, buffer_rows, fractions, points, edge, local, fars, prev):
    n_own, _, width = points.shape
    held = LOW + n_own + HIGH
    hbm = pl.BlockSpec(memory_space=pl.ANY)
    smem = pl.BlockSpec(memory_space=pltpu.SMEM)
    args = [table, buffer_rows, fractions, points, edge, local, *fars]
    if prev is not None:
        args.append(prev)
    moved = (held + n_own) * rows * width * points.dtype.itemsize
    return pl.pallas_call(
        functools.partial(place_kernel, rows, len(fars), prev is not None),
        out_shape=jax.ShapeDtypeStruct(points.shape, points.dtype),
        in_specs=[smem] * 3 + [hbm] * (len(args) - 3),
        out_specs=hbm,
        scratch_shapes=[
            pltpu.VMEM((held, rows, width), points.dtype),
            pltpu.VMEM((n_own, rows, width), points.dtype),
            pltpu.SemaphoreType.DMA((COL_BLOCKS, 4)),
            pltpu.SemaphoreType.DMA((COL_BLOCKS,)),
        ],
        input_output_aliases={} if prev is None else {len(args) - 1: 0},
        cost_estimate=pl.CostEstimate(
            flops=4 * n_own * rows * width, bytes_accessed=moved, transcendentals=0
        ),
    )(*args)


def squares(start, end):
    step = end.astype(jnp.float32) - start.astype(jnp.float32)
    return jnp.sum(step * step, axis=(1, 2))


def finish(all_squares, first_point, n_own, n_points, source_segment, numerators):
    index = jnp.arange(n_points, dtype=jnp.int32)
    lengths = jnp.where(index < n_points - 1, jnp.sqrt(all_squares), 0.0)
    arcs = jnp.concatenate([jnp.zeros((1,), jnp.float32), jnp.cumsum(lengths)[:-1]])
    total = arcs[n_points - 1]
    target = total * (
        source_segment.astype(jnp.float32) + numerators.astype(jnp.float32) / 65536.0
    ) / (n_points - 1)
    fractions = (target - arcs[source_segment]) / lengths[source_segment]
    arc = lax.dynamic_slice(arcs, (first_point,), (n_own,)) / total
    return fractions, arc


def chain_device(points, source_segment, numerators):
    n_own, n_rows, _ = points.shape
    device_index = lax.axis_index("seg")
    device_count = lax.axis_size("seg")
    first_point = device_index * n_own
    n_points = device_count * n_own
    forward = [(i, i + 1) for i in range(device_count - 1)]
    backward = [(b, a) for a, b in forward]
    rows = TILE_ROWS
    n_chunks = n_rows // rows

    first = lax.ppermute(points[:1], "seg", backward)
    lows, highs = [], []
    for c in range(n_chunks):
        at = slice(c * rows, (c + 1) * rows)
        lows.append(lax.ppermute(points[n_own - LOW :, at], "seg", forward))
        highs.append(lax.ppermute(points[1:HIGH, at], "seg", backward))
    inner = squares(points[:-1], points[1:])
    edge = squares(points[n_own - 1 :], first)
    own_squares = lax.psum(jnp.concatenate([inner, edge]), "par")
    all_squares = lax.all_gather(own_squares, "seg", axis=0, tiled=True)
    fractions, arc = finish(
        all_squares, first_point, n_own, n_points, source_segment, numerators
    )
    buffer_rows = source_segment - first_point + LOW
    out = None
    for c in range(n_chunks):
        table = jnp.array(
            [c * rows, c * rows, 0, LOW + n_own, LOW + n_own + 1, 0], jnp.int32
        )
        out = place(
            rows, table, buffer_rows, fractions, points, first,
            lows[c], (highs[c],), out,
        )
    return (out, arc)


def paired_device(points, source_segment, numerators):
    n_own, n_rows, width = points.shape
    device_index = lax.axis_index("seg")
    count = lax.axis_size("seg")
    pairs = count // 2
    side = device_index % 2
    even = side == 0
    first_point = device_index * n_own
    n_points = count * n_own
    rows = TILE_ROWS
    steps = n_rows // rows
    half = n_rows // 2

    local_pairs = [(2 * k, 2 * k + 1) for k in range(pairs)]
    local_pairs += [(b, a) for a, b in local_pairs]
    far_pairs = [(2 * k + 1, 2 * k + 2) for k in range(pairs - 1)]
    far_pairs += [(b, a) for a, b in far_pairs]

    def relayed(source, step):
        k = source // 2
        return (k if source % 2 == 0 else pairs - 1 - k) * steps > step * pairs

    relay_of = lambda source: source + 1 if source % 2 == 0 else source - 1
    hop1 = [[(a, relay_of(a)) for a, b in far_pairs if relayed(a, s)] for s in range(steps)]
    hop2 = [[(relay_of(a), b) for a, b in far_pairs if relayed(a, s)] for s in range(steps)]
    direct = [[(a, b) for a, b in far_pairs if not relayed(a, s)] for s in range(steps)]

    def border(to_next):
        start = jnp.where(to_next, n_own - 1, 0), jnp.where(to_next, half, 0), 0
        return lax.dynamic_slice(points, start, (1, half, width))

    def row_of(is_even, step):
        return jnp.where(is_even, step, steps - 1 - step) * rows

    edge_far = lax.ppermute(border(~even), "seg", far_pairs)
    edge_local = lax.ppermute(border(even), "seg", local_pairs)

    far_payload, local_payload = [], []
    for s in range(steps):
        n_far = 3 if s < steps // 2 else 2
        n_local = 5 - n_far
        far_start = jnp.where(even, 3 - n_far, n_own - 3)
        far_payload.append(
            lax.dynamic_slice(
                points, (far_start, row_of(~even, s), 0), (n_far, rows, width)
            )
        )
        local_start = jnp.where(even, n_own - 3, 3 - n_local)
        local_payload.append(
            lax.dynamic_slice(
                points, (local_start, row_of(~even, s), 0), (n_local, rows, width)
            )
        )
    middle, relay, far, local = {}, {}, {}, {}
    for s in range(steps):
        if hop1[s]:
            middle[s] = lax.ppermute(far_payload[s], "seg", hop1[s])
        local[s] = lax.ppermute(local_payload[s], "seg", local_pairs)
    for s in range(steps):
        if direct[s]:
            far[s] = lax.ppermute(far_payload[s], "seg", direct[s])
        if hop2[s]:
            relay[s] = lax.ppermute(middle[s], "seg", hop2[s])

    from_prev = jnp.where(even, edge_far, edge_local)
    from_next = jnp.where(even, edge_local, edge_far)
    partial = jnp.concatenate(
        [
            squares(from_prev, points[:1, half:]),
            squares(points[:-1], points[1:]),
            squares(points[n_own - 1 :, :half], from_next),
        ]
    )
    partial = lax.psum(partial, "par")
    spread = lax.dynamic_update_slice(
        jnp.zeros((n_points + 1,), jnp.float32), partial, (first_point,)
    )
    shift = 1
    while shift < pairs:
        ring = [(2 * k, 2 * ((k - shift) % pairs)) for k in range(pairs)]
        ring += [(2 * k + 1, 2 * ((k + shift) % pairs) + 1) for k in range(pairs)]
        spread = spread + lax.ppermute(spread, "seg", ring)
        shift *= 2
    cross = [(2 * k, 2 * ((k - 1) % pairs) + 1) for k in range(pairs)]
    cross += [(2 * k + 1, 2 * ((k + 1) % pairs)) for k in range(pairs)]
    spread = spread + lax.ppermute(spread, "seg", cross)
    fractions, arc = finish(
        spread[1:], first_point, n_own, n_points, source_segment, numerators
    )
    buffer_rows = source_segment - first_point + LOW

    target_relayed = np.zeros((steps, count), np.int32)
    for s in range(steps):
        for _, b in hop2[s]:
            target_relayed[s, b] = 1
    out = None
    for s in range(steps):
        row = row_of(even, s)
        if s < steps // 2:
            at_local = jnp.where(even, LOW + n_own + 1, 0)
            at_edge = jnp.where(even, LOW + n_own, LOW - 1)
            at_far = jnp.where(even, 0, LOW + n_own)
            edge = edge_local
        else:
            at_local = jnp.where(even, LOW + n_own, 0)
            at_edge = jnp.where(even, LOW - 1, LOW + n_own)
            at_far = jnp.where(even, 0, LOW + n_own + 1)
            edge = edge_far
        flag = jnp.asarray(target_relayed[s])[device_index]
        table = jnp.stack(
            [row, row % half, at_local, at_edge, at_far, flag]
        ).astype(jnp.int32)
        fars = tuple(d[s] for d in (far, relay) if s in d)
        out = place(
            rows, table, buffer_rows, fractions, points, edge,
            local[s], fars, out,
        )
    return (out, arc)


def is_paired(mesh):
    names = mesh.axis_names
    devices = np.moveaxis(mesh.devices, names.index("seg"), 0)
    devices = devices.reshape(devices.shape[0], -1)[:, 0]
    count = len(devices)
    pairs = count // 2
    if count % 2 or pairs < 2 or pairs & (pairs - 1):
        return False
    places = [getattr(device, "coords", None) for device in devices]
    if any(place is None for place in places):
        return False
    return all(
        (place[0], place[2]) == (i % 2, i // 2) and place[1] == places[0][1]
        for i, place in enumerate(places)
    )


def solution(mesh):
    paired = is_paired(mesh)

    def body(*args):
        return (paired_device if paired else chain_device)(*args)

    return jax.shard_map(
        body,
        mesh=mesh,
        in_specs=(P("seg", "par", None), P("seg"), P("seg")),
        out_specs=(P("seg", "par", None), P("seg")),
        check_vma=False,
    )
```

```python
import functools

import jax
import jax.numpy as jnp
import numpy as np
from jax import lax
from jax.experimental import pallas as pl
from jax.experimental.pallas import tpu as pltpu
from jax.sharding import PartitionSpec as P


BLOCK_COLS = 1024
LOW = 3
HIGH = 3
CHAIN_CHUNKS = 4
CUTS = (0, 2, 4, 7, 8)
COL, EDGE_COL, AT_LOCAL, AT_EDGE, AT_FAR, EDGE_IS_NEXT, RELAYED = range(7)


def place_kernel(
    cols, n_edges, n_fars, has_prev, table, buffer_rows, fractions, points, local, *rest
):
    edges, fars = rest[:n_edges], rest[n_edges : n_edges + n_fars]
    out, buf, res, in_sem, out_sem = rest[n_edges + n_fars + has_prev :]
    n_own = points.shape[0]
    width = min(BLOCK_COLS, cols)
    blocks = cols // width
    col = pl.multiple_of(table[COL], width)
    edge_col = pl.multiple_of(table[EDGE_COL], width)

    def into(src, start, count, c, k):
        dst = buf.at[pl.ds(start, count), :, pl.ds(c * width, width)]
        return pltpu.make_async_copy(src, dst, in_sem.at[c, k])

    def own_in(c):
        at = pl.ds(col + c * width, width)
        return into(points.at[:, :, at], LOW, n_own, c, 0)

    def local_in(c):
        at = pl.ds(c * width, width)
        return into(local.at[:, :, at], table[AT_LOCAL], local.shape[0], c, 1)

    def edge_in(c, edge):
        at = pl.ds(edge_col + c * width, width)
        return into(edge.at[:, :, at], table[AT_EDGE], 1, c, 2)

    def far_in(c, far):
        at = pl.ds(c * width, width)
        return into(far.at[:, :, at], table[AT_FAR], far.shape[0], c, 3)

    def start_one(copy, c, refs, entry):
        if len(refs) == 1:
            copy(c, refs[0]).start()
            return

        @pl.when(table[entry] == 0)
        def _():
            copy(c, refs[0]).start()

        @pl.when(table[entry] == 1)
        def _():
            copy(c, refs[1]).start()

    def res_out(c):
        return pltpu.make_async_copy(
            res.at[:, :, pl.ds(c * width, width)],
            out.at[:, :, pl.ds(col + c * width, width)],
            out_sem.at[c],
        )

    for c in range(blocks):
        own_in(c).start()
        local_in(c).start()
        start_one(edge_in, c, edges, EDGE_IS_NEXT)
        start_one(far_in, c, fars, RELAYED)
    for c in range(blocks):
        own_in(c).wait()
        local_in(c).wait()
        edge_in(c, edges[0]).wait()
        far_in(c, fars[0]).wait()
        at = pl.ds(c * width, width)

        @pl.loop(0, n_own)
        def _(j):
            start = buf[buffer_rows[j], :, at].astype(jnp.float32)
            end = buf[buffer_rows[j] + 1, :, at].astype(jnp.float32)
            res[j, :, at] = (start + fractions[j] * (end - start)).astype(res.dtype)

        res_out(c).start()
    for c in range(blocks):
        res_out(c).wait()


def place(cols, table, buffer_rows, fractions, points, local, edges, fars, prev):
    n_own, rows, _ = points.shape
    held = LOW + n_own + HIGH
    hbm = pl.BlockSpec(memory_space=pl.ANY)
    smem = pl.BlockSpec(memory_space=pltpu.SMEM)
    args = [table, buffer_rows, fractions, points, local, *edges, *fars]
    if prev is not None:
        args.append(prev)
    moved = (held + n_own) * rows * cols * points.dtype.itemsize
    blocks = cols // min(BLOCK_COLS, cols)
    return pl.pallas_call(
        functools.partial(
            place_kernel, cols, len(edges), len(fars), prev is not None
        ),
        out_shape=jax.ShapeDtypeStruct(points.shape, points.dtype),
        in_specs=[smem] * 3 + [hbm] * (len(args) - 3),
        out_specs=hbm,
        scratch_shapes=[
            pltpu.VMEM((held, rows, cols), points.dtype),
            pltpu.VMEM((n_own, rows, cols), points.dtype),
            pltpu.SemaphoreType.DMA((blocks, 4)),
            pltpu.SemaphoreType.DMA((blocks,)),
        ],
        input_output_aliases={} if prev is None else {len(args) - 1: 0},
        cost_estimate=pl.CostEstimate(
            flops=4 * n_own * rows * cols, bytes_accessed=moved, transcendentals=0
        ),
        compiler_params=pltpu.CompilerParams(vmem_limit_bytes=moved + (4 << 20)),
    )(*args)


def squares(start, end):
    step = end.astype(jnp.float32) - start.astype(jnp.float32)
    return jnp.sum(step * step, axis=(1, 2))


def finish(all_squares, first_point, n_own, n_points, source_segment, numerators):
    index = jnp.arange(n_points, dtype=jnp.int32)
    lengths = jnp.where(index < n_points - 1, jnp.sqrt(all_squares), 0.0)
    arcs = jnp.concatenate([jnp.zeros((1,), jnp.float32), jnp.cumsum(lengths)[:-1]])
    total = arcs[n_points - 1]
    target = total * (
        source_segment.astype(jnp.float32) + numerators.astype(jnp.float32) / 65536.0
    ) / (n_points - 1)
    fractions = (target - arcs[source_segment]) / lengths[source_segment]
    arc = lax.dynamic_slice(arcs, (first_point,), (n_own,)) / total
    return fractions, arc


def chain_device(points, source_segment, numerators):
    n_own, _, width = points.shape
    device_index = lax.axis_index("seg")
    device_count = lax.axis_size("seg")
    first_point = device_index * n_own
    n_points = device_count * n_own
    forward = [(i, i + 1) for i in range(device_count - 1)]
    backward = [(b, a) for a, b in forward]
    cols = width // CHAIN_CHUNKS

    first = lax.ppermute(points[:1], "seg", backward)
    lows, highs = [], []
    for c in range(CHAIN_CHUNKS):
        at = slice(c * cols, (c + 1) * cols)
        lows.append(lax.ppermute(points[n_own - LOW :, :, at], "seg", forward))
        highs.append(lax.ppermute(points[1:HIGH, :, at], "seg", backward))
    inner = squares(points[:-1], points[1:])
    edge = squares(points[n_own - 1 :], first)
    own_squares = lax.psum(jnp.concatenate([inner, edge]), "par")
    all_squares = lax.all_gather(own_squares, "seg", axis=0, tiled=True)
    fractions, arc = finish(
        all_squares, first_point, n_own, n_points, source_segment, numerators
    )
    buffer_rows = source_segment - first_point + LOW
    out = None
    for c in range(CHAIN_CHUNKS):
        table = jnp.array(
            [c * cols, c * cols, 0, LOW + n_own, LOW + n_own + 1, 0, 0], jnp.int32
        )
        out = place(
            cols, table, buffer_rows, fractions, points, lows[c],
            (first,), (highs[c],), out,
        )
    return (out, arc)


def paired_device(points, source_segment, numerators):
    n_own, _, width = points.shape
    device_index = lax.axis_index("seg")
    count = lax.axis_size("seg")
    pairs = count // 2
    even = device_index % 2 == 0
    first_point = device_index * n_own
    n_points = count * n_own
    steps = len(CUTS) - 1
    half = width // 2
    cuts = [width * cut // CUTS[-1] for cut in CUTS]

    forward = [(i, i + 1) for i in range(count - 1)]
    backward = [(b, a) for a, b in forward]
    local_pairs = [(2 * k, 2 * k + 1) for k in range(pairs)]
    local_pairs += [(b, a) for a, b in local_pairs]
    far_pairs = [(2 * k + 1, 2 * k + 2) for k in range(pairs - 1)]
    far_pairs += [(b, a) for a, b in far_pairs]

    def relayed(source, step):
        k = source // 2 if source % 2 == 0 else pairs - 1 - source // 2
        return k * steps > step * pairs

    def beside(source):
        return source + 1 if source % 2 == 0 else source - 1

    hop1, hop2, direct = [], [], []
    for s in range(steps):
        through = [(a, b) for a, b in far_pairs if relayed(a, s)]
        hop1.append([(a, beside(a)) for a, b in through])
        hop2.append([(beside(a), b) for a, b in through])
        direct.append([(a, b) for a, b in far_pairs if not relayed(a, s)])

    from_prev = lax.ppermute(points[n_own - 1 :, :, half:], "seg", forward)
    from_next = lax.ppermute(points[:1, :, :half], "seg", backward)

    def span(to_even, step):
        start, end = cuts[step], cuts[step + 1]
        return slice(start, end) if to_even else slice(width - end, width - start)

    far_payload, local_payload = [], []
    for s in range(steps):
        n_far = 3 if s < steps // 2 else 2
        n_local = 5 - n_far
        on, back = span(True, s), span(False, s)
        far_payload.append(
            jnp.where(
                even,
                points[3 - n_far : 3, :, back],
                points[n_own - 3 : n_own - 3 + n_far, :, on],
            )
        )
        local_payload.append(
            jnp.where(
                even,
                points[n_own - 3 : n_own - 3 + n_local, :, back],
                points[3 - n_local : 3, :, on],
            )
        )
    middle, relay, far, local = {}, {}, {}, {}
    for s in range(steps):
        if hop1[s]:
            middle[s] = lax.ppermute(far_payload[s], "seg", hop1[s])
        local[s] = lax.ppermute(local_payload[s], "seg", local_pairs)
    for s in range(steps):
        if direct[s]:
            far[s] = lax.ppermute(far_payload[s], "seg", direct[s])
        if hop2[s]:
            relay[s] = lax.ppermute(middle[s], "seg", hop2[s])

    partial = jnp.concatenate(
        [
            squares(from_prev, points[:1, :, half:]),
            squares(points[:-1], points[1:]),
            squares(points[n_own - 1 :, :, :half], from_next),
        ]
    )
    partial = lax.psum(partial, "par")
    spread = lax.dynamic_update_slice(
        jnp.zeros((n_points + 1,), jnp.float32), partial, (first_point,)
    )
    shift = 1
    while shift < pairs:
        ring = [(2 * k, 2 * ((k - shift) % pairs)) for k in range(pairs)]
        ring += [(2 * k + 1, 2 * ((k + shift) % pairs) + 1) for k in range(pairs)]
        spread = spread + lax.ppermute(spread, "seg", ring)
        shift *= 2
    cross = [(2 * k, 2 * ((k - 1) % pairs) + 1) for k in range(pairs)]
    cross += [(2 * k + 1, 2 * ((k + 1) % pairs)) for k in range(pairs)]
    spread = spread + lax.ppermute(spread, "seg", cross)
    fractions, arc = finish(
        spread[1:], first_point, n_own, n_points, source_segment, numerators
    )
    buffer_rows = source_segment - first_point + LOW

    tables = np.zeros((count, steps, 7), np.int32)
    for s in range(steps):
        early = s < steps // 2
        for i in range(count):
            at_even = i % 2 == 0
            col = span(at_even, s).start
            next_edge = at_even == early
            tables[i, s, COL] = col
            tables[i, s, EDGE_COL] = col % half
            tables[i, s, EDGE_IS_NEXT] = next_edge
            tables[i, s, AT_EDGE] = LOW + n_own if next_edge else LOW - 1
            tables[i, s, AT_LOCAL] = LOW + n_own + early if at_even else 0
            tables[i, s, AT_FAR] = 0 if at_even else LOW + n_own + (not early)
        for _, b in hop2[s]:
            tables[b, s, RELAYED] = 1
    table = lax.dynamic_index_in_dim(jnp.asarray(tables), device_index, 0, False)
    out = None
    for s in range(steps):
        fars = tuple(d[s] for d in (far, relay) if s in d)
        out = place(
            cuts[s + 1] - cuts[s], table[s], buffer_rows, fractions,
            points, local[s], (from_prev, from_next), fars, out,
        )
    return (out, arc)


def is_paired(mesh):
    names = mesh.axis_names
    devices = np.moveaxis(mesh.devices, names.index("seg"), 0)
    devices = devices.reshape(devices.shape[0], -1)[:, 0]
    count = len(devices)
    pairs = count // 2
    if count % 2 or pairs != len(CUTS) - 1:
        return False
    places = [getattr(device, "coords", None) for device in devices]
    if any(place is None for place in places):
        return False
    return all(
        (place[0], place[2]) == (i % 2, i // 2) and place[1] == places[0][1]
        for i, place in enumerate(places)
    )


def solution(mesh):
    paired = is_paired(mesh)

    def body(*args):
        return (paired_device if paired else chain_device)(*args)

    return jax.shard_map(
        body,
        mesh=mesh,
        in_specs=(P("seg", "par", None), P("seg"), P("seg")),
        out_specs=(P("seg", "par", None), P("seg")),
        check_vma=False,
    )
```
